1024 devices in a mesh: lat: 16 (over x, y_lo, core), lev: 64 (over z, y_hi).
Axes of the slice: x: 4, y: 8 (y_hi: 4, y_lo: 2; y = y_hi * 2 + y_lo), z: 16, core: 2. Of those that a mesh axis runs over, the one named last changes fastest.
Arguments:
- fields: bfloat16 [6, 128, 128, 1152], P(None, 'lev', 'lat'), may hold values from -6 to 6
- courant: bfloat16 [128, 128, 1152], P('lev', 'lat'), may hold values from -0.8984375 to 0.8984375
- filter_matrix: bfloat16 [1152, 1152], replicated, may hold values from -0.1875 to 0.1875
- polar_mask: int32 [128], P('lat'), may hold values from 0 to 1, as said below
- band_start: int32 [128], replicated, may hold values from 0 to 124, as said below
- remap_weights: float32 [128, 128, 4], P('lat'), may hold values from 0.05 to 0.5
Outputs:
- remapped: bfloat16 [6, 128, 128, 1152], P(None, 'lev', 'lat')
The draws below stay inside these ranges and needn't reach their ends.
Inputs may be any that keep to these rules, and one draw needn't show every extreme that they name: `polar_mask`: 1 on a run of 16 to 32 latitudes at each pole, 0 elsewhere. band_start[0] is 0 and band_start[127] is 124.
All inputs are finite; a program needn't handle non-finite values.
Results may differ from the reference program's by a relative error of at most 0.0052.
Values may be sent and summed in bfloat16 or wider, within the bound.
A program may use at most 32 MiB of HBM per device.

```python
import jax
import jax.numpy as jnp
from jax import lax

NLON = 1152
F = 6
BAND = 4
NLAT = 128
NLEV = 128
DRIFT = 32


def draw_polar_mask(key, part):
    key_south, key_north = jax.random.split(key)
    cut_south = jax.random.randint(key_south, (), NLAT // 8, NLAT // 4 + 1)
    cut_north = jax.random.randint(key_north, (), NLAT // 8, NLAT // 4 + 1)
    row_index = jnp.arange(NLAT, dtype=jnp.int32)
    return ((row_index < cut_south) | (row_index >= NLAT - cut_north)).astype(jnp.int32)


def draw_band_start(key, part):
    drift_draw = jax.random.randint(key, (NLEV,), -DRIFT, DRIFT + 1)
    level_index = jnp.arange(NLEV, dtype=jnp.int32)
    start_level = jnp.clip(level_index + drift_draw, 0, NLEV - BAND)
    start_level = start_level.at[0].set(0).at[NLEV - 1].set(NLEV - BAND)
    return start_level.astype(jnp.int32)


def level_of(key, shape, cuts, low, top_value):
    def one(dim, shards_of):
        heights = jax.random.uniform(jax.random.fold_in(jax.random.fold_in(key, 6), dim), (shards_of,), jnp.float32, low / len(cuts), top_value / len(cuts))
        return jnp.repeat(jnp.exp(heights), shape[dim] // shards_of).reshape((-1,) + (1,) * (len(shape) - dim - 1))

    level = one(*cuts[0])
    for cut in cuts[1:]:
        level = level * one(*cut)
    return level


def gaussian(own_key, shape, width, limit, cuts=(), held_as=jnp.bfloat16):
    level = level_of(own_key, shape, cuts, -0.22, 0.18) if cuts else 1.0
    values = jax.random.normal(own_key, shape, jnp.float32) * width * level
    return jnp.minimum(jnp.maximum(values, -limit), limit).astype(held_as)


def setup_inputs(seed: int = 0) -> dict:
    seeds = jax.random.split(jax.random.key(seed), 7)
    fields = gaussian(seeds[0], (F, NLEV, NLAT, NLON), 1.0, 6.0, ((1, 64), (2, 16)))
    courant = jnp.clip(jax.random.uniform(seeds[1], (NLEV, NLAT, NLON), jnp.float32, -0.8984375, 0.8984375) * level_of(seeds[1], (NLEV, NLAT, NLON), ((0, 64), (1, 16)), -0.4, 0.0), -0.8984375, 0.8984375).astype(jnp.bfloat16)
    filter_matrix = gaussian(seeds[2], (NLON, NLON), NLON ** -0.5, 0.1875)
    polar_mask = draw_polar_mask(jax.random.fold_in(seeds[6], 71), 0)
    band_start = draw_band_start(jax.random.fold_in(seeds[6], 71), 0)
    remap_weights = jnp.clip(0.05 + 0.45 * jax.random.uniform(seeds[5], (NLAT, NLEV, BAND), jnp.float32) ** level_of(seeds[5], (NLAT, NLEV, BAND), ((0, 16),), -0.2, 0.2), 0.05, 0.5)
    return {"fields": fields, "courant": courant, "filter_matrix": filter_matrix, "polar_mask": polar_mask, "band_start": band_start, "remap_weights": remap_weights}


def band_matrix(band_start, remap_weights):
    level_total = band_start.shape[0]
    band_width = remap_weights.shape[2]
    source_level = jnp.arange(level_total, dtype=jnp.int32)[None, :, None]
    target_start = band_start.astype(jnp.int32)[None, None, :] + jnp.arange(band_width, dtype=jnp.int32)[:, None, None]
    one_hot = (source_level == target_start).astype(jnp.float32)
    return jnp.einsum("jtb,bst->jst", remap_weights.astype(jnp.float32), one_hot, precision=lax.Precision.HIGHEST)


def reference(fields, courant, filter_matrix, polar_mask, band_start, remap_weights):
    lat_total = fields.shape[2]
    lon_total = fields.shape[3]
    speed_pad = jnp.pad(courant.astype(jnp.float32), ((0, 0), (2, 2), (0, 0)))
    face_index = jnp.arange(lat_total + 1, dtype=jnp.int32) - 1
    face_live = ((face_index >= 0) & (face_index <= lat_total - 2)).astype(jnp.float32)[None, :, None]
    face_speed = 0.5 * (speed_pad[:, 1:lat_total + 2] + speed_pad[:, 2:lat_total + 3]) * face_live
    matrix = band_matrix(band_start, remap_weights)
    polar_rows = (polar_mask == 1)[None, :, None]

    def one_field(field_in):
        padded = jnp.pad(field_in.astype(jnp.float32), ((0, 0), (2, 2), (0, 0)))
        face_flux = face_speed * (7.0 * (padded[:, 1:lat_total + 2] + padded[:, 2:lat_total + 3])
                                  - (padded[:, 0:lat_total + 1] + padded[:, 3:lat_total + 4])) / 12.0
        moved_field = padded[:, 2:lat_total + 2] - (face_flux[:, 1:] - face_flux[:, :-1])
        moved_low = moved_field.astype(jnp.bfloat16)
        correction = jnp.dot(moved_low.reshape(-1, lon_total), filter_matrix,
                             preferred_element_type=jnp.float32).reshape(moved_field.shape)
        filtered = (moved_field + jnp.where(polar_rows, correction, 0.0)).astype(jnp.bfloat16)
        result = jnp.einsum("sji,jst->tji", filtered.astype(jnp.float32), matrix, precision=lax.Precision.HIGHEST)
        return result.astype(jnp.bfloat16)

    return lax.map(one_field, fields)
```

```python
import functools

import jax
import jax.numpy as jnp
from jax import lax
from jax.experimental import pallas as pl
from jax.experimental.pallas import tpu as pltpu
from jax.sharding import PartitionSpec as P

LANES = 128
MESH = pl.DeviceIdType.MESH


def kernel(
    fields_hbm, courant_hbm, matrix_hbm, mask_ref, start_ref, weight_ref, out_ref,
    fields_ref, courant_ref, matrix_ref, field_low, field_high, courant_low, courant_high,
    extended, speed, moved, moved_low, filtered, columns, spread, remapped,
    load_sem, halo_send, halo_recv, column_send, column_recv, back_send, back_recv,
    *, lat_count, lev_count,
):
    field_count, level_rows, lat_rows, lon_total = fields_hbm.shape
    planes = field_count * level_rows
    tiles = lon_total // LANES
    units = field_count * tiles
    level_total = level_rows * lev_count
    band_width = weight_ref.shape[1]
    lat = lax.axis_index("lat")
    lev = lax.axis_index("lev")

    def owner_of(q):
        return lax.div((q + 1) * lev_count + units - 1, units) - 1

    unit = lax.div(lev * units, lev_count)
    active = lax.div((lev + 1) * units, lev_count) > unit
    unit_field = lax.div(unit, tiles)
    unit_lanes = pl.ds(pl.multiple_of(lax.rem(unit, tiles) * LANES, LANES), LANES)
    polar = (lat < lat_count // 4) | (lat >= lat_count - lat_count // 4)
    has_low = lat > 0
    has_high = lat < lat_count - 1

    loads = [
        pltpu.make_async_copy(fields_hbm, fields_ref, load_sem.at[0]),
        pltpu.make_async_copy(courant_hbm, courant_ref, load_sem.at[1]),
    ]
    for load in loads:
        load.start()
    load_matrix = pltpu.make_async_copy(matrix_hbm, matrix_ref, load_sem.at[2])
    load_matrix.start()

    barrier = pltpu.get_barrier_semaphore()

    @pl.when(has_low)
    def _():
        pl.semaphore_signal(barrier, inc=1, device_id={"lat": lat - 1}, device_id_type=MESH)

    @pl.when(has_high)
    def _():
        pl.semaphore_signal(barrier, inc=1, device_id={"lat": lat + 1}, device_id_type=MESH)

    def greet(i, carry):
        peer = lax.rem(lev + i, lev_count)
        pl.semaphore_signal(barrier, inc=1, device_id={"lev": peer}, device_id_type=MESH)
        return carry

    lax.fori_loop(1, lev_count, greet, 0)

    @pl.when(active)
    def _():
        group = 8

        def spread_group(g, weights):
            rolled = []
            for b in range(band_width):
                for k in range(group):
                    spread[g * group + k, b] = jnp.broadcast_to(
                        weights[b][:, k : k + 1], (lat_rows, LANES)
                    )
                rolled.append(pltpu.roll(weights[b], LANES - group, 1))
            return tuple(rolled)

        lax.fori_loop(
            0,
            level_total // group,
            spread_group,
            tuple(weight_ref[:, b, :] for b in range(band_width)),
        )

    for load in loads:
        load.wait()

    pl.semaphore_wait(
        barrier, lev_count - 1 + jnp.where(has_low, 1, 0) + jnp.where(has_high, 1, 0)
    )

    def halo_copies(up):
        rows = pl.ds(lat_rows - 2, 2) if up else pl.ds(0, 2)
        to = lat + 1 if up else lat - 1
        side = 0 if up else 1
        pairs = (
            (fields_ref, field_low if up else field_high),
            (courant_ref, courant_low if up else courant_high),
        )
        return [
            pltpu.make_async_remote_copy(
                src_ref=source.at[..., rows, :],
                dst_ref=target,
                send_sem=halo_send.at[side, k],
                recv_sem=halo_recv.at[side, k],
                device_id={"lat": to},
                device_id_type=MESH,
            )
            for k, (source, target) in enumerate(pairs)
        ]

    @pl.when(has_high)
    def _():
        for copy in halo_copies(True):
            copy.start()

    @pl.when(has_low)
    def _():
        for copy in halo_copies(False):
            copy.start()

    own = pl.ds(8, lat_rows)
    for f in range(field_count):
        for l in range(level_rows):
            extended[f * level_rows + l, own, :] = fields_ref[f, l].astype(jnp.float32)
    for l in range(level_rows):
        speed[l, own, :] = courant_ref[l].astype(jnp.float32)

    def fill(rows, field_halo, courant_halo, there, side):
        @pl.when(there)
        def _():
            for copy in halo_copies(side == 0):
                copy.wait_recv()
            for f in range(field_count):
                for l in range(level_rows):
                    extended[f * level_rows + l, rows, :] = field_halo[f, l].astype(jnp.float32)
            for l in range(level_rows):
                speed[l, rows, :] = courant_halo[l].astype(jnp.float32)

        @pl.when(jnp.logical_not(there))
        def _():
            for p in range(planes):
                extended[p, rows, :] = jnp.zeros((2, lon_total), jnp.float32)
            for l in range(level_rows):
                speed[l, rows, :] = jnp.zeros((2, lon_total), jnp.float32)

    fill(pl.ds(6, 2), field_low, courant_low, has_low, 0)
    fill(pl.ds(8 + lat_rows, 2), field_high, courant_high, has_high, 1)

    row = lax.broadcasted_iota(jnp.int32, (lat_rows, lon_total), 0)
    live_low = jnp.where((row > 0) | has_low, 0.5 / 12.0, 0.0)
    live_high = jnp.where((row < lat_rows - 1) | has_high, 0.5 / 12.0, 0.0)

    def at(ref, p, shift):
        return ref[p, pl.ds(8 + shift, lat_rows), :]

    for l in range(level_rows):
        centre = at(speed, l, 0)
        low = (at(speed, l, -1) + centre) * live_low
        high = (centre + at(speed, l, 1)) * live_high
        for f in range(field_count):
            p = f * level_rows + l
            q = [at(extended, p, shift) for shift in (-2, -1, 0, 1, 2)]
            flux_low = low * (7.0 * (q[1] + q[2]) - (q[0] + q[3]))
            flux_high = high * (7.0 * (q[2] + q[3]) - (q[1] + q[4]))
            result = q[2] - (flux_high - flux_low)
            moved[p] = result

    load_matrix.wait()

    @pl.when(polar)
    def _():
        for f in range(field_count):
            both = moved[pl.ds(f * level_rows, level_rows)]
            moved_low[pl.ds(f * level_rows * lat_rows, level_rows * lat_rows), :] = both.reshape(
                level_rows * lat_rows, lon_total
            ).astype(jnp.bfloat16)

    small_row = lax.broadcasted_iota(jnp.int32, (lat_rows, LANES), 0)
    mask = jnp.zeros((lat_rows, LANES), jnp.int32)
    for j in range(lat_rows):
        mask = jnp.where(small_row == j, mask_ref[j], mask)

    def column_copy(q, lanes, f):
        return pltpu.make_async_remote_copy(
            src_ref=filtered.at[f, :, :, lanes],
            dst_ref=columns.at[pl.ds(lev * level_rows, level_rows)],
            send_sem=column_send,
            recv_sem=column_recv,
            device_id={"lev": owner_of(q)},
            device_id_type=MESH,
        )

    for first in range(0, tiles, 2):
        count = min(2, tiles - first)
        width = count * LANES
        lanes = pl.ds(first * LANES, width)

        @pl.when(polar)
        def _():
            correction = jnp.dot(
                moved_low[...], matrix_ref[:, lanes], preferred_element_type=jnp.float32
            ).reshape(field_count, level_rows, lat_rows, width)
            wide_mask = jnp.concatenate([mask] * count, axis=1) == 1
            kept = jnp.where(wide_mask[None, None], correction, 0.0)
            total = moved[:, :, lanes].reshape(kept.shape) + kept
            filtered[:, :, :, lanes] = total.astype(jnp.bfloat16)

        @pl.when(jnp.logical_not(polar))
        def _():
            filtered[:, :, :, lanes] = (
                moved[:, :, lanes]
                .reshape(field_count, level_rows, lat_rows, width)
                .astype(jnp.bfloat16)
            )

        def send_field(i, carry):
            f = lax.rem(i + lev, field_count)
            for k in range(count):
                q = f * tiles + first + k
                there = pl.ds((first + k) * LANES, LANES)

                @pl.when(owner_of(q) != lev)
                def _():
                    column_copy(q, there, f).start()

            return carry

        lax.fori_loop(0, field_count, send_field, 0)

    def sized(count):
        return columns.at[pl.ds(0, count * level_rows)]

    @pl.when(active)
    def _():
        columns[pl.ds(lev * level_rows, level_rows)] = filtered[unit_field, :, :, unit_lanes]
        pltpu.make_async_copy(sized(lev_count - 1), sized(lev_count - 1), column_recv).wait()

        def target(t):
            begin = start_ref[t]
            total = jnp.zeros((lat_rows, LANES), jnp.float32)
            for b in range(band_width):
                total = total + spread[t, b] * columns[begin + b].astype(jnp.float32)
            return total.astype(jnp.bfloat16)

        def send_back(i, carry):
            peer = lax.rem(lev + i, lev_count)
            place = pl.ds(peer * level_rows, level_rows)
            for l in range(level_rows):
                remapped[peer * level_rows + l] = target(peer * level_rows + l)
            pltpu.make_async_remote_copy(
                src_ref=remapped.at[place],
                dst_ref=out_ref.at[unit_field, :, :, unit_lanes],
                send_sem=back_send,
                recv_sem=back_recv,
                device_id={"lev": peer},
                device_id_type=MESH,
            ).start()
            return carry

        lax.fori_loop(1, lev_count, send_back, 0)
        for l in range(level_rows):
            out_ref[unit_field, l, :, unit_lanes] = target(lev * level_rows + l)
        pltpu.make_async_copy(sized(lev_count - 1), sized(lev_count - 1), back_send).wait()
        pltpu.make_async_copy(sized(units - 1), sized(units - 1), column_send).wait()
        pltpu.make_async_copy(sized(units - 1), sized(units - 1), back_recv).wait()

    @pl.when(jnp.logical_not(active))
    def _():
        pltpu.make_async_copy(sized(units), sized(units), column_send).wait()
        pltpu.make_async_copy(sized(units), sized(units), back_recv).wait()

    @pl.when(has_high)
    def _():
        for copy in halo_copies(True):
            copy.wait_send()

    @pl.when(has_low)
    def _():
        for copy in halo_copies(False):
            copy.wait_send()


def on_device(lat_count, lev_count, fields, courant, matrix, mask, start, weights):
    field_count, level_rows, lat_rows, lon_total = fields.shape
    planes = field_count * level_rows
    level_total = level_rows * lev_count
    band_width = weights.shape[2]
    bf16, f32 = jnp.bfloat16, jnp.float32
    anywhere = pl.BlockSpec(memory_space=pl.ANY)
    smem = pl.BlockSpec(memory_space=pltpu.SMEM)
    vmem = pl.BlockSpec(memory_space=pltpu.VMEM)
    return pl.pallas_call(
        functools.partial(kernel, lat_count=lat_count, lev_count=lev_count),
        out_shape=jax.ShapeDtypeStruct(fields.shape, bf16),
        in_specs=[anywhere, anywhere, anywhere, smem, smem, vmem],
        out_specs=vmem,
        scratch_shapes=[
            pltpu.VMEM(fields.shape, bf16),
            pltpu.VMEM(courant.shape, bf16),
            pltpu.VMEM(matrix.shape, bf16),
            pltpu.VMEM((field_count, level_rows, 2, lon_total), bf16),
            pltpu.VMEM((field_count, level_rows, 2, lon_total), bf16),
            pltpu.VMEM((level_rows, 2, lon_total), bf16),
            pltpu.VMEM((level_rows, 2, lon_total), bf16),
            pltpu.VMEM((planes, lat_rows + 16, lon_total), f32),
            pltpu.VMEM((level_rows, lat_rows + 16, lon_total), f32),
            pltpu.VMEM((planes, lat_rows, lon_total), f32),
            pltpu.VMEM((planes * lat_rows, lon_total), bf16),
            pltpu.VMEM(fields.shape, bf16),
            pltpu.VMEM((level_total, lat_rows, LANES), bf16),
            pltpu.VMEM((level_total, band_width, lat_rows, LANES), f32),
            pltpu.VMEM((level_total, lat_rows, LANES), bf16),
            pltpu.SemaphoreType.DMA((3,)),
            pltpu.SemaphoreType.DMA((2, 2)),
            pltpu.SemaphoreType.DMA((2, 2)),
            pltpu.SemaphoreType.DMA,
            pltpu.SemaphoreType.DMA,
            pltpu.SemaphoreType.DMA,
            pltpu.SemaphoreType.DMA,
        ],
        compiler_params=pltpu.CompilerParams(
            collective_id=0, has_side_effects=True, vmem_limit_bytes=32 << 20
        ),
    )(fields, courant, matrix, mask, start, jnp.transpose(weights, (0, 2, 1)))


def solution(mesh):
    step = functools.partial(on_device, mesh.shape["lat"], mesh.shape["lev"])
    placed = (
        P(None, "lev", "lat", None),
        P("lev", "lat", None),
        P(),
        P("lat"),
        P(),
        P("lat", None, None),
    )
    return jax.shard_map(
        step, mesh=mesh, in_specs=placed, out_specs=P(None, "lev", "lat", None), check_vma=False
    )
```

```python
import functools

import jax
import jax.numpy as jnp
from jax import lax
from jax.experimental import pallas as pl
from jax.experimental.pallas import tpu as pltpu
from jax.sharding import PartitionSpec as P

LANES = 128
MESH = pl.DeviceIdType.MESH


def kernel(
    fields_hbm, courant_hbm, matrix_hbm, mask_ref, start_ref, weight_ref, out_ref,
    fields_ref, courant_ref, matrix_ref, field_low, field_high, courant_low, courant_high,
    extended, speed, moved, moved_low, filtered, columns, spread, remapped,
    load_sem, ready, halo_send, halo_recv, column_send, column_recv, back_send, back_recv,
    *, lat_count, lev_count, group_size,
):
    field_count, level_rows, lat_rows, lon_total = fields_hbm.shape
    planes = field_count * level_rows
    tiles = lon_total // LANES
    units = field_count * tiles
    level_total = level_rows * lev_count
    band_width = weight_ref.shape[1]
    lat = lax.axis_index("lat")
    lev = lax.axis_index("lev")

    spare = lev_count - units
    first_spare = units // 2

    def owns(d):
        return (d < first_spare) | (d >= first_spare + spare)

    def unit_of(d):
        return jnp.where(d < first_spare, d, d - spare)

    active = owns(lev)
    unit = jnp.where(active, unit_of(lev), 0)
    group = lax.div(lev, group_size)
    groups = lev_count // group_size
    ready_count = (group + 1) * group_size
    unit_field = lax.div(unit, tiles)
    unit_lanes = pl.ds(pl.multiple_of(lax.rem(unit, tiles) * LANES, LANES), LANES)
    polar = (lat < lat_count // 4) | (lat >= lat_count - lat_count // 4)
    has_low = lat > 0
    has_high = lat < lat_count - 1

    loads = [
        pltpu.make_async_copy(fields_hbm, fields_ref, load_sem.at[0]),
        pltpu.make_async_copy(courant_hbm, courant_ref, load_sem.at[1]),
    ]
    for load in loads:
        load.start()
    load_matrix = pltpu.make_async_copy(matrix_hbm, matrix_ref, load_sem.at[2])
    load_matrix.start()

    barrier = pltpu.get_barrier_semaphore()

    @pl.when(has_low)
    def _():
        pl.semaphore_signal(barrier, inc=1, device_id={"lat": lat - 1}, device_id_type=MESH)

    @pl.when(has_high)
    def _():
        pl.semaphore_signal(barrier, inc=1, device_id={"lat": lat + 1}, device_id_type=MESH)

    def greet(peer, carry):
        @pl.when(peer != lev)
        def _():
            pl.semaphore_signal(barrier, inc=1, device_id={"lev": peer}, device_id_type=MESH)

        return carry

    lax.fori_loop(group * group_size, lev_count, greet, 0)

    for load in loads:
        load.wait()

    pl.semaphore_wait(
        barrier, ready_count - 1 + jnp.where(has_low, 1, 0) + jnp.where(has_high, 1, 0)
    )

    def halo_copies(up):
        rows = pl.ds(lat_rows - 2, 2) if up else pl.ds(0, 2)
        to = lat + 1 if up else lat - 1
        side = 0 if up else 1
        pairs = (
            (fields_ref, field_low if up else field_high),
            (courant_ref, courant_low if up else courant_high),
        )
        return [
            pltpu.make_async_remote_copy(
                src_ref=source.at[..., rows, :],
                dst_ref=target,
                send_sem=halo_send.at[side, k],
                recv_sem=halo_recv.at[side, k],
                device_id={"lat": to},
                device_id_type=MESH,
            )
            for k, (source, target) in enumerate(pairs)
        ]

    @pl.when(has_high)
    def _():
        for copy in halo_copies(True):
            copy.start()

    @pl.when(has_low)
    def _():
        for copy in halo_copies(False):
            copy.start()

    def announce(peer, carry):
        pl.semaphore_signal(
            ready.at[group], inc=1, device_id={"lev": peer}, device_id_type=MESH
        )
        return carry

    lax.fori_loop(0, group * group_size, announce, 0)

    own = pl.ds(8, lat_rows)
    for f in range(field_count):
        for l in range(level_rows):
            extended[f * level_rows + l, own, :] = fields_ref[f, l].astype(jnp.float32)
    for l in range(level_rows):
        speed[l, own, :] = courant_ref[l].astype(jnp.float32)

    def fill(rows, field_halo, courant_halo, there, side):
        @pl.when(there)
        def _():
            for copy in halo_copies(side == 0):
                copy.wait_recv()
            for f in range(field_count):
                for l in range(level_rows):
                    extended[f * level_rows + l, rows, :] = field_halo[f, l].astype(jnp.float32)
            for l in range(level_rows):
                speed[l, rows, :] = courant_halo[l].astype(jnp.float32)

        @pl.when(jnp.logical_not(there))
        def _():
            for p in range(planes):
                extended[p, rows, :] = jnp.zeros((2, lon_total), jnp.float32)
            for l in range(level_rows):
                speed[l, rows, :] = jnp.zeros((2, lon_total), jnp.float32)

    fill(pl.ds(6, 2), field_low, courant_low, has_low, 0)
    fill(pl.ds(8 + lat_rows, 2), field_high, courant_high, has_high, 1)

    row = lax.broadcasted_iota(jnp.int32, (lat_rows, lon_total), 0)
    live_low = jnp.where((row > 0) | has_low, 0.5 / 12.0, 0.0)
    live_high = jnp.where((row < lat_rows - 1) | has_high, 0.5 / 12.0, 0.0)

    def at(ref, p, shift):
        return ref[p, pl.ds(8 + shift, lat_rows), :]

    for l in range(level_rows):
        centre = at(speed, l, 0)
        low = (at(speed, l, -1) + centre) * live_low
        high = (centre + at(speed, l, 1)) * live_high
        for f in range(field_count):
            p = f * level_rows + l
            q = [at(extended, p, shift) for shift in (-2, -1, 0, 1, 2)]
            flux_low = low * (7.0 * (q[1] + q[2]) - (q[0] + q[3]))
            flux_high = high * (7.0 * (q[2] + q[3]) - (q[1] + q[4]))
            result = q[2] - (flux_high - flux_low)
            moved[p] = result

    load_matrix.wait()

    @pl.when(polar)
    def _():
        for f in range(field_count):
            both = moved[pl.ds(f * level_rows, level_rows)]
            moved_low[pl.ds(f * level_rows * lat_rows, level_rows * lat_rows), :] = both.reshape(
                level_rows * lat_rows, lon_total
            ).astype(jnp.bfloat16)

    small_row = lax.broadcasted_iota(jnp.int32, (lat_rows, LANES), 0)
    mask = jnp.zeros((lat_rows, LANES), jnp.int32)
    for j in range(lat_rows):
        mask = jnp.where(small_row == j, mask_ref[j], mask)

    for first in range(0, tiles, 2):
        count = min(2, tiles - first)
        width = count * LANES
        lanes = pl.ds(first * LANES, width)

        @pl.when(polar)
        def _():
            correction = jnp.dot(
                moved_low[...], matrix_ref[:, lanes], preferred_element_type=jnp.float32
            ).reshape(field_count, level_rows, lat_rows, width)
            wide_mask = jnp.concatenate([mask] * count, axis=1) == 1
            kept = jnp.where(wide_mask[None, None], correction, 0.0)
            total = moved[:, :, lanes].reshape(kept.shape) + kept
            filtered[:, :, :, lanes] = total.astype(jnp.bfloat16)

        @pl.when(jnp.logical_not(polar))
        def _():
            filtered[:, :, :, lanes] = (
                moved[:, :, lanes]
                .reshape(field_count, level_rows, lat_rows, width)
                .astype(jnp.bfloat16)
            )

    def send_to(d):
        @pl.when(owns(d) & (d != lev))
        def _():
            q = unit_of(d)
            lanes = pl.ds(pl.multiple_of(lax.rem(q, tiles) * LANES, LANES), LANES)
            pltpu.make_async_remote_copy(
                src_ref=filtered.at[lax.div(q, tiles), :, :, lanes],
                dst_ref=columns.at[pl.ds(lev * level_rows, level_rows)],
                send_sem=column_send,
                recv_sem=column_recv,
                device_id={"lev": d},
                device_id_type=MESH,
            ).start()

    def send_ready(i, carry):
        step = lax.div(i + 1, 2)
        step = jnp.where(lax.rem(i, 2) == 1, step, ready_count - step)
        send_to(lax.rem(lev + lev_count // 2 + step, ready_count))
        return carry

    lax.fori_loop(0, ready_count, send_ready, 0)

    def send_later(h, carry):
        pl.semaphore_wait(ready.at[h], group_size)

        def each(k, carry):
            send_to(h * group_size + k)
            return carry

        return lax.fori_loop(0, group_size, each, carry)

    lax.fori_loop(group + 1, groups, send_later, 0)

    @pl.when(active)
    def _():
        group = 8

        def spread_group(g, weights):
            rolled = []
            for b in range(band_width):
                for k in range(group):
                    spread[g * group + k, b] = jnp.broadcast_to(
                        weights[b][:, k : k + 1], (lat_rows, LANES)
                    )
                rolled.append(pltpu.roll(weights[b], LANES - group, 1))
            return tuple(rolled)

        lax.fori_loop(
            0,
            level_total // group,
            spread_group,
            tuple(weight_ref[:, b, :] for b in range(band_width)),
        )

    def sized(count):
        return columns.at[pl.ds(0, count * level_rows)]

    @pl.when(active)
    def _():
        columns[pl.ds(lev * level_rows, level_rows)] = filtered[unit_field, :, :, unit_lanes]
        pltpu.make_async_copy(sized(lev_count - 1), sized(lev_count - 1), column_recv).wait()

        def target(t):
            begin = start_ref[t]
            total = jnp.zeros((lat_rows, LANES), jnp.float32)
            for b in range(band_width):
                total = total + spread[t, b] * columns[begin + b].astype(jnp.float32)
            return total.astype(jnp.bfloat16)

        def send_back(i, carry):
            peer = jnp.where(i <= lev, i - 1, i)
            place = pl.ds(peer * level_rows, level_rows)
            for l in range(level_rows):
                remapped[peer * level_rows + l] = target(peer * level_rows + l)
            pltpu.make_async_remote_copy(
                src_ref=remapped.at[place],
                dst_ref=out_ref.at[unit_field, :, :, unit_lanes],
                send_sem=back_send,
                recv_sem=back_recv,
                device_id={"lev": peer},
                device_id_type=MESH,
            ).start()
            return carry

        lax.fori_loop(1, lev_count, send_back, 0)
        for l in range(level_rows):
            out_ref[unit_field, l, :, unit_lanes] = target(lev * level_rows + l)
        pltpu.make_async_copy(sized(lev_count - 1), sized(lev_count - 1), back_send).wait()
        pltpu.make_async_copy(sized(units - 1), sized(units - 1), column_send).wait()
        pltpu.make_async_copy(sized(units - 1), sized(units - 1), back_recv).wait()

    @pl.when(jnp.logical_not(active))
    def _():
        pltpu.make_async_copy(sized(units), sized(units), column_send).wait()
        pltpu.make_async_copy(sized(units), sized(units), back_recv).wait()

    @pl.when(has_high)
    def _():
        for copy in halo_copies(True):
            copy.wait_send()

    @pl.when(has_low)
    def _():
        for copy in halo_copies(False):
            copy.wait_send()


def on_device(lat_count, lev_count, fields, courant, matrix, mask, start, weights):
    field_count, level_rows, lat_rows, lon_total = fields.shape
    planes = field_count * level_rows
    group_size = 4
    level_total = level_rows * lev_count
    band_width = weights.shape[2]
    bf16, f32 = jnp.bfloat16, jnp.float32
    anywhere = pl.BlockSpec(memory_space=pl.ANY)
    smem = pl.BlockSpec(memory_space=pltpu.SMEM)
    vmem = pl.BlockSpec(memory_space=pltpu.VMEM)
    return pl.pallas_call(
        functools.partial(
            kernel, lat_count=lat_count, lev_count=lev_count, group_size=group_size
        ),
        out_shape=jax.ShapeDtypeStruct(fields.shape, bf16),
        in_specs=[anywhere, anywhere, anywhere, smem, smem, vmem],
        out_specs=vmem,
        scratch_shapes=[
            pltpu.VMEM(fields.shape, bf16),
            pltpu.VMEM(courant.shape, bf16),
            pltpu.VMEM(matrix.shape, bf16),
            pltpu.VMEM((field_count, level_rows, 2, lon_total), bf16),
            pltpu.VMEM((field_count, level_rows, 2, lon_total), bf16),
            pltpu.VMEM((level_rows, 2, lon_total), bf16),
            pltpu.VMEM((level_rows, 2, lon_total), bf16),
            pltpu.VMEM((planes, lat_rows + 16, lon_total), f32),
            pltpu.VMEM((level_rows, lat_rows + 16, lon_total), f32),
            pltpu.VMEM((planes, lat_rows, lon_total), f32),
            pltpu.VMEM((planes * lat_rows, lon_total), bf16),
            pltpu.VMEM(fields.shape, bf16),
            pltpu.VMEM((level_total, lat_rows, LANES), bf16),
            pltpu.VMEM((level_total, band_width, lat_rows, LANES), f32),
            pltpu.VMEM((level_total, lat_rows, LANES), bf16),
            pltpu.SemaphoreType.DMA((3,)),
            pltpu.SemaphoreType.REGULAR((lev_count // group_size,)),
            pltpu.SemaphoreType.DMA((2, 2)),
            pltpu.SemaphoreType.DMA((2, 2)),
            pltpu.SemaphoreType.DMA,
            pltpu.SemaphoreType.DMA,
            pltpu.SemaphoreType.DMA,
            pltpu.SemaphoreType.DMA,
        ],
        compiler_params=pltpu.CompilerParams(
            collective_id=0, has_side_effects=True, vmem_limit_bytes=63 << 20
        ),
    )(fields, courant, matrix, mask, start, jnp.transpose(weights, (0, 2, 1)))


def solution(mesh):
    step = functools.partial(on_device, mesh.shape["lat"], mesh.shape["lev"])
    placed = (
        P(None, "lev", "lat", None),
        P("lev", "lat", None),
        P(),
        P("lat"),
        P(),
        P("lat", None, None),
    )
    return jax.shard_map(
        step, mesh=mesh, in_specs=placed, out_specs=P(None, "lev", "lat", None), check_vma=False
    )
```

```python
import functools

import jax
import jax.numpy as jnp
from jax import lax
from jax.experimental import pallas as pl
from jax.experimental.pallas import tpu as pltpu
from jax.sharding import PartitionSpec as P

LANES = 128
MESH = pl.DeviceIdType.MESH


def kernel(
    fields_hbm, courant_hbm, matrix_hbm, mask_hbm, start_hbm, weight_hbm, out_ref,
    mask_ref, start_ref, weight_ref, fields_ref, courant_ref, matrix_ref, field_low, field_high, courant_low, courant_high,
    extended, speed, moved, moved_low, filtered, columns, spread, remapped,
    load_sem, place_sem, ready, halo_send, halo_recv, column_send, column_recv, back_send, back_recv,
    *, lat_count, lev_count, group_size,
):
    field_count, level_rows, lat_rows, lon_total = fields_hbm.shape
    planes = field_count * level_rows
    tiles = lon_total // LANES
    units = field_count * tiles
    level_total = level_rows * lev_count
    band_width = weight_ref.shape[1]
    lat = lax.axis_index("lat")
    lev = lax.axis_index("lev")

    spare = lev_count - units
    whole_groups = lev_count // group_size - spare
    slot = group_size // 2
    full = whole_groups * group_size

    def owns(d):
        return (d < full) | (lax.rem(d, group_size) != slot)

    def unit_of(d):
        later = lax.div(d, group_size) - whole_groups
        passed = later + jnp.where(lax.rem(d, group_size) > slot, 1, 0)
        return d - jnp.where(d < full, 0, passed)

    active = owns(lev)
    unit = jnp.where(active, unit_of(lev), 0)
    group = lax.div(lev, group_size)
    groups = lev_count // group_size
    ready_count = (group + 1) * group_size
    unit_field = lax.div(unit, tiles)
    unit_lanes = pl.ds(pl.multiple_of(lax.rem(unit, tiles) * LANES, LANES), LANES)
    polar = (lat < lat_count // 4) | (lat >= lat_count - lat_count // 4)
    has_low = lat > 0
    has_high = lat < lat_count - 1

    loads = [
        pltpu.make_async_copy(fields_hbm, fields_ref, load_sem.at[0]),
        pltpu.make_async_copy(courant_hbm, courant_ref, load_sem.at[1]),
    ]
    for load in loads:
        load.start()
    late_loads = [
        pltpu.make_async_copy(source, target, load_sem.at[2 + k])
        for k, (source, target) in enumerate(
            (
                (mask_hbm, mask_ref),
                (matrix_hbm, matrix_ref),
                (start_hbm, start_ref),
                (weight_hbm, weight_ref),
            )
        )
    ]
    for load in late_loads:
        load.start()

    barrier = pltpu.get_barrier_semaphore()

    @pl.when(has_low)
    def _():
        pl.semaphore_signal(barrier, inc=1, device_id={"lat": lat - 1}, device_id_type=MESH)

    @pl.when(has_high)
    def _():
        pl.semaphore_signal(barrier, inc=1, device_id={"lat": lat + 1}, device_id_type=MESH)

    def greet(peer, carry):
        @pl.when(peer != lev)
        def _():
            pl.semaphore_signal(barrier, inc=1, device_id={"lev": peer}, device_id_type=MESH)

        return carry

    lax.fori_loop(group * group_size, lev_count, greet, 0)

    for load in loads:
        load.wait()

    pl.semaphore_wait(
        barrier, ready_count - 1 + jnp.where(has_low, 1, 0) + jnp.where(has_high, 1, 0)
    )

    def halo_copies(up):
        rows = pl.ds(lat_rows - 2, 2) if up else pl.ds(0, 2)
        to = lat + 1 if up else lat - 1
        side = 0 if up else 1
        pairs = (
            (fields_ref, field_low if up else field_high),
            (courant_ref, courant_low if up else courant_high),
        )
        return [
            pltpu.make_async_remote_copy(
                src_ref=source.at[..., rows, :],
                dst_ref=target,
                send_sem=halo_send.at[side, k],
                recv_sem=halo_recv.at[side, k],
                device_id={"lat": to},
                device_id_type=MESH,
            )
            for k, (source, target) in enumerate(pairs)
        ]

    @pl.when(has_high)
    def _():
        for copy in halo_copies(True):
            copy.start()

    @pl.when(has_low)
    def _():
        for copy in halo_copies(False):
            copy.start()

    def announce(peer, carry):
        pl.semaphore_signal(
            ready.at[group], inc=1, device_id={"lev": peer}, device_id_type=MESH
        )
        return carry

    lax.fori_loop(0, group * group_size, announce, 0)

    own = pl.ds(8, lat_rows)
    for f in range(field_count):
        for l in range(level_rows):
            extended[f * level_rows + l, own, :] = fields_ref[f, l].astype(jnp.float32)
    for l in range(level_rows):
        speed[l, own, :] = courant_ref[l].astype(jnp.float32)

    def fill(rows, field_halo, courant_halo, there, side):
        @pl.when(there)
        def _():
            for copy in halo_copies(side == 0):
                copy.wait_recv()
            for f in range(field_count):
                for l in range(level_rows):
                    extended[f * level_rows + l, rows, :] = field_halo[f, l].astype(jnp.float32)
            for l in range(level_rows):
                speed[l, rows, :] = courant_halo[l].astype(jnp.float32)

        @pl.when(jnp.logical_not(there))
        def _():
            for p in range(planes):
                extended[p, rows, :] = jnp.zeros((2, lon_total), jnp.float32)
            for l in range(level_rows):
                speed[l, rows, :] = jnp.zeros((2, lon_total), jnp.float32)

    fill(pl.ds(6, 2), field_low, courant_low, has_low, 0)
    fill(pl.ds(8 + lat_rows, 2), field_high, courant_high, has_high, 1)

    row = lax.broadcasted_iota(jnp.int32, (lat_rows, lon_total), 0)
    live_low = jnp.where((row > 0) | has_low, 0.5 / 12.0, 0.0)
    live_high = jnp.where((row < lat_rows - 1) | has_high, 0.5 / 12.0, 0.0)

    def at(ref, p, shift):
        return ref[p, pl.ds(8 + shift, lat_rows), :]

    for l in range(level_rows):
        centre = at(speed, l, 0)
        low = (at(speed, l, -1) + centre) * live_low
        high = (centre + at(speed, l, 1)) * live_high
        for f in range(field_count):
            p = f * level_rows + l
            q = [at(extended, p, shift) for shift in (-2, -1, 0, 1, 2)]
            flux_low = low * (7.0 * (q[1] + q[2]) - (q[0] + q[3]))
            flux_high = high * (7.0 * (q[2] + q[3]) - (q[1] + q[4]))
            result = q[2] - (flux_high - flux_low)
            moved[p] = result

    for load in late_loads:
        load.wait()

    @pl.when(polar)
    def _():
        for f in range(field_count):
            both = moved[pl.ds(f * level_rows, level_rows)]
            moved_low[pl.ds(f * level_rows * lat_rows, level_rows * lat_rows), :] = both.reshape(
                level_rows * lat_rows, lon_total
            ).astype(jnp.bfloat16)

    small_row = lax.broadcasted_iota(jnp.int32, (lat_rows, LANES), 0)
    mask = jnp.zeros((lat_rows, LANES), jnp.int32)
    for j in range(lat_rows):
        mask = jnp.where(small_row == j, mask_ref[j], mask)

    def owner_of(q):
        rest = jnp.maximum(q - full, 0)
        place = lax.rem(rest, group_size - 1)
        place = place + jnp.where(place >= slot, 1, 0)
        later = full + lax.div(rest, group_size - 1) * group_size + place
        return jnp.where(q < full, q, later)

    def send(q, d):
        @pl.when(d != lev)
        def _():
            lanes = pl.ds(pl.multiple_of(lax.rem(q, tiles) * LANES, LANES), LANES)
            pltpu.make_async_remote_copy(
                src_ref=filtered.at[lax.div(q, tiles), :, :, lanes],
                dst_ref=columns.at[pl.ds(lev * level_rows, level_rows)],
                send_sem=column_send,
                recv_sem=column_recv,
                device_id={"lev": d},
                device_id_type=MESH,
            ).start()

    def send_to(d):
        @pl.when(owns(d))
        def _():
            send(unit_of(d), d)

    far_field = lax.div(
        lev * field_count, lev_count
    )

    for first in range(0, tiles, 2):
        count = min(2, tiles - first)
        width = count * LANES
        lanes = pl.ds(first * LANES, width)

        @pl.when(polar)
        def _():
            correction = jnp.dot(
                moved_low[...], matrix_ref[:, lanes], preferred_element_type=jnp.float32
            ).reshape(field_count, level_rows, lat_rows, width)
            wide_mask = jnp.concatenate([mask] * count, axis=1) == 1
            kept = jnp.where(wide_mask[None, None], correction, 0.0)
            total = moved[:, :, lanes].reshape(kept.shape) + kept
            filtered[:, :, :, lanes] = total.astype(jnp.bfloat16)

        @pl.when(jnp.logical_not(polar))
        def _():
            filtered[:, :, :, lanes] = (
                moved[:, :, lanes]
                .reshape(field_count, level_rows, lat_rows, width)
                .astype(jnp.bfloat16)
            )

        def send_block(i, carry):
            f = lax.rem(far_field + i, field_count)
            for k in range(count):
                q = f * tiles + first + k

                @pl.when(owner_of(q) < ready_count)
                def _():
                    send(q, owner_of(q))

            return carry

        lax.fori_loop(0, field_count, send_block, 0)

    def send_later(h, carry):
        pl.semaphore_wait(ready.at[h], group_size)

        def each(k, carry):
            send_to(h * group_size + k)
            return carry

        return lax.fori_loop(0, group_size, each, carry)

    lax.fori_loop(group + 1, groups, send_later, 0)

    @pl.when(active)
    def _():
        group = 8

        def spread_group(g, weights):
            rolled = []
            for b in range(band_width):
                for k in range(group):
                    spread[g * group + k, b] = jnp.broadcast_to(
                        weights[b][:, k : k + 1], (lat_rows, LANES)
                    )
                rolled.append(pltpu.roll(weights[b], LANES - group, 1))
            return tuple(rolled)

        lax.fori_loop(
            0,
            level_total // group,
            spread_group,
            tuple(weight_ref[:, b, :] for b in range(band_width)),
        )

    def sized(count):
        return columns.at[pl.ds(0, count * level_rows)]

    @pl.when(active)
    def _():
        columns[pl.ds(lev * level_rows, level_rows)] = filtered[unit_field, :, :, unit_lanes]
        pltpu.make_async_copy(sized(lev_count - 1), sized(lev_count - 1), column_recv).wait()

        def target(t):
            begin = start_ref[t]
            total = jnp.zeros((lat_rows, LANES), jnp.float32)
            for b in range(band_width):
                total = total + spread[t, b] * columns[begin + b].astype(jnp.float32)
            return total.astype(jnp.bfloat16)

        def send_back(i, carry):
            peer = jnp.where(i <= lev, i - 1, i)
            place = pl.ds(peer * level_rows, level_rows)
            for l in range(level_rows):
                remapped[peer * level_rows + l] = target(peer * level_rows + l)
            pltpu.make_async_remote_copy(
                src_ref=remapped.at[place],
                dst_ref=out_ref.at[unit_field, :, :, unit_lanes],
                send_sem=back_send,
                recv_sem=back_recv,
                device_id={"lev": peer},
                device_id_type=MESH,
            ).start()
            return carry

        lax.fori_loop(1, lev_count, send_back, 0)
        for l in range(level_rows):
            remapped[lev * level_rows + l] = target(lev * level_rows + l)
        keep = pltpu.make_async_copy(
            remapped.at[pl.ds(lev * level_rows, level_rows)],
            out_ref.at[unit_field, :, :, unit_lanes],
            place_sem,
        )
        keep.start()
        pltpu.make_async_copy(sized(lev_count - 1), sized(lev_count - 1), back_send).wait()
        pltpu.make_async_copy(sized(units - 1), sized(units - 1), column_send).wait()
        pltpu.make_async_copy(sized(units - 1), sized(units - 1), back_recv).wait()
        keep.wait()

    @pl.when(jnp.logical_not(active))
    def _():
        pltpu.make_async_copy(sized(units), sized(units), column_send).wait()
        pltpu.make_async_copy(sized(units), sized(units), back_recv).wait()

    @pl.when(has_high)
    def _():
        for copy in halo_copies(True):
            copy.wait_send()

    @pl.when(has_low)
    def _():
        for copy in halo_copies(False):
            copy.wait_send()


def on_device(lat_count, lev_count, fields, courant, matrix, mask, start, weights):
    field_count, level_rows, lat_rows, lon_total = fields.shape
    planes = field_count * level_rows
    group_size = 4
    level_total = level_rows * lev_count
    band_width = weights.shape[2]
    bf16, f32 = jnp.bfloat16, jnp.float32
    anywhere = pl.BlockSpec(memory_space=pl.ANY)
    return pl.pallas_call(
        functools.partial(
            kernel, lat_count=lat_count, lev_count=lev_count, group_size=group_size
        ),
        out_shape=jax.ShapeDtypeStruct(fields.shape, bf16),
        in_specs=[anywhere] * 6,
        out_specs=anywhere,
        scratch_shapes=[
            pltpu.SMEM(mask.shape, jnp.int32),
            pltpu.SMEM(start.shape, jnp.int32),
            pltpu.VMEM((weights.shape[0], band_width, level_total), f32),
            pltpu.VMEM(fields.shape, bf16),
            pltpu.VMEM(courant.shape, bf16),
            pltpu.VMEM(matrix.shape, bf16),
            pltpu.VMEM((field_count, level_rows, 2, lon_total), bf16),
            pltpu.VMEM((field_count, level_rows, 2, lon_total), bf16),
            pltpu.VMEM((level_rows, 2, lon_total), bf16),
            pltpu.VMEM((level_rows, 2, lon_total), bf16),
            pltpu.VMEM((planes, lat_rows + 16, lon_total), f32),
            pltpu.VMEM((level_rows, lat_rows + 16, lon_total), f32),
            pltpu.VMEM((planes, lat_rows, lon_total), f32),
            pltpu.VMEM((planes * lat_rows, lon_total), bf16),
            pltpu.VMEM(fields.shape, bf16),
            pltpu.VMEM((level_total, lat_rows, LANES), bf16),
            pltpu.VMEM((level_total, band_width, lat_rows, LANES), f32),
            pltpu.VMEM((level_total, lat_rows, LANES), bf16),
            pltpu.SemaphoreType.DMA((6,)),
            pltpu.SemaphoreType.DMA,
            pltpu.SemaphoreType.REGULAR((lev_count // group_size,)),
            pltpu.SemaphoreType.DMA((2, 2)),
            pltpu.SemaphoreType.DMA((2, 2)),
            pltpu.SemaphoreType.DMA,
            pltpu.SemaphoreType.DMA,
            pltpu.SemaphoreType.DMA,
            pltpu.SemaphoreType.DMA,
        ],
        compiler_params=pltpu.CompilerParams(
            collective_id=0, has_side_effects=True, vmem_limit_bytes=63 << 20
        ),
    )(fields, courant, matrix, mask, start, jnp.transpose(weights, (0, 2, 1)))


def solution(mesh):
    step = functools.partial(on_device, mesh.shape["lat"], mesh.shape["lev"])
    placed = (
        P(None, "lev", "lat", None),
        P("lev", "lat", None),
        P(),
        P("lat"),
        P(),
        P("lat", None, None),
    )
    return jax.shard_map(
        step, mesh=mesh, in_specs=placed, out_specs=P(None, "lev", "lat", None), check_vma=False
    )
```

```python
import functools

import jax
import jax.numpy as jnp
from jax import lax
from jax.experimental import pallas as pl
from jax.experimental.pallas import tpu as pltpu
from jax.sharding import PartitionSpec as P

LANES = 128
MESH = pl.DeviceIdType.MESH


def kernel(
    fields_hbm, courant_hbm, matrix_hbm, mask_hbm, start_hbm, weight_hbm, out_ref,
    mask_ref, start_ref, weight_ref, fields_ref, courant_ref, matrix_ref, field_low, field_high, courant_low, courant_high,
    extended, speed, moved, moved_low, filtered, columns, spread, remapped,
    load_sem, place_sem, ready, halo_send, halo_recv, column_send, column_recv, back_send, back_recv,
    *, lat_count, lev_count, group_size,
):
    field_count, level_rows, lat_rows, lon_total = fields_hbm.shape
    planes = field_count * level_rows
    tiles = lon_total // LANES
    units = field_count * tiles
    level_total = level_rows * lev_count
    band_width = weight_ref.shape[1]
    lat = lax.axis_index("lat")
    lev = lax.axis_index("lev")

    spare = lev_count - units
    whole_groups = lev_count // group_size - spare
    slot = group_size // 2
    full = whole_groups * group_size

    def owns(d):
        return (d < full) | (lax.rem(d, group_size) != slot)

    def unit_of(d):
        later = lax.div(d, group_size) - whole_groups
        passed = later + jnp.where(lax.rem(d, group_size) > slot, 1, 0)
        return d - jnp.where(d < full, 0, passed)

    active = owns(lev)
    unit = jnp.where(active, unit_of(lev), 0)
    group = lax.div(lev, group_size)
    groups = lev_count // group_size
    ready_count = (group + 1) * group_size
    unit_field = lax.div(unit, tiles)
    unit_lanes = pl.ds(pl.multiple_of(lax.rem(unit, tiles) * LANES, LANES), LANES)
    polar = (lat < lat_count // 4) | (lat >= lat_count - lat_count // 4)
    has_low = lat > 0
    has_high = lat < lat_count - 1

    loads = [
        pltpu.make_async_copy(fields_hbm, fields_ref, load_sem.at[0]),
        pltpu.make_async_copy(courant_hbm, courant_ref, load_sem.at[1]),
    ]
    for load in loads:
        load.start()
    late_loads = [
        pltpu.make_async_copy(source, target, load_sem.at[2 + k])
        for k, (source, target) in enumerate(
            (
                (mask_hbm, mask_ref),
                (matrix_hbm, matrix_ref),
                (start_hbm, start_ref),
                (weight_hbm, weight_ref),
            )
        )
    ]
    for load in late_loads:
        load.start()

    barrier = pltpu.get_barrier_semaphore()

    @pl.when(has_low)
    def _():
        pl.semaphore_signal(barrier, inc=1, device_id={"lat": lat - 1}, device_id_type=MESH)

    @pl.when(has_high)
    def _():
        pl.semaphore_signal(barrier, inc=1, device_id={"lat": lat + 1}, device_id_type=MESH)

    def greet(peer, carry):
        @pl.when(peer != lev)
        def _():
            pl.semaphore_signal(barrier, inc=1, device_id={"lev": peer}, device_id_type=MESH)

        return carry

    lax.fori_loop(group * group_size, lev_count, greet, 0)

    for load in loads:
        load.wait()

    pl.semaphore_wait(
        barrier, ready_count - 1 + jnp.where(has_low, 1, 0) + jnp.where(has_high, 1, 0)
    )

    def halo_copies(up):
        rows = pl.ds(lat_rows - 2, 2) if up else pl.ds(0, 2)
        to = lat + 1 if up else lat - 1
        side = 0 if up else 1
        pairs = (
            (fields_ref, field_low if up else field_high),
            (courant_ref, courant_low if up else courant_high),
        )
        return [
            pltpu.make_async_remote_copy(
                src_ref=source.at[..., rows, :],
                dst_ref=target,
                send_sem=halo_send.at[side, k],
                recv_sem=halo_recv.at[side, k],
                device_id={"lat": to},
                device_id_type=MESH,
            )
            for k, (source, target) in enumerate(pairs)
        ]

    @pl.when(has_high)
    def _():
        for copy in halo_copies(True):
            copy.start()

    @pl.when(has_low)
    def _():
        for copy in halo_copies(False):
            copy.start()

    def announce(peer, carry):
        pl.semaphore_signal(
            ready.at[group], inc=1, device_id={"lev": peer}, device_id_type=MESH
        )
        return carry

    lax.fori_loop(0, group * group_size, announce, 0)

    own = pl.ds(8, lat_rows)
    for f in range(field_count):
        for l in range(level_rows):
            extended[f * level_rows + l, own, :] = fields_ref[f, l].astype(jnp.float32)
    for l in range(level_rows):
        speed[l, own, :] = courant_ref[l].astype(jnp.float32)

    def fill(rows, field_halo, courant_halo, there, side):
        @pl.when(there)
        def _():
            for copy in halo_copies(side == 0):
                copy.wait_recv()
            for f in range(field_count):
                for l in range(level_rows):
                    extended[f * level_rows + l, rows, :] = field_halo[f, l].astype(jnp.float32)
            for l in range(level_rows):
                speed[l, rows, :] = courant_halo[l].astype(jnp.float32)

        @pl.when(jnp.logical_not(there))
        def _():
            for p in range(planes):
                extended[p, rows, :] = jnp.zeros((2, lon_total), jnp.float32)
            for l in range(level_rows):
                speed[l, rows, :] = jnp.zeros((2, lon_total), jnp.float32)

    fill(pl.ds(6, 2), field_low, courant_low, has_low, 0)
    fill(pl.ds(8 + lat_rows, 2), field_high, courant_high, has_high, 1)

    row = lax.broadcasted_iota(jnp.int32, (lat_rows, lon_total), 0)
    live_low = jnp.where((row > 0) | has_low, 0.5 / 12.0, 0.0)
    live_high = jnp.where((row < lat_rows - 1) | has_high, 0.5 / 12.0, 0.0)

    def at(ref, p, shift):
        return ref[p, pl.ds(8 + shift, lat_rows), :]

    for l in range(level_rows):
        centre = at(speed, l, 0)
        low = (at(speed, l, -1) + centre) * live_low
        high = (centre + at(speed, l, 1)) * live_high
        for f in range(field_count):
            p = f * level_rows + l
            q = [at(extended, p, shift) for shift in (-2, -1, 0, 1, 2)]
            flux_low = low * (7.0 * (q[1] + q[2]) - (q[0] + q[3]))
            flux_high = high * (7.0 * (q[2] + q[3]) - (q[1] + q[4]))
            result = q[2] - (flux_high - flux_low)
            moved[p] = result

    for load in late_loads:
        load.wait()

    @pl.when(polar)
    def _():
        for f in range(field_count):
            both = moved[pl.ds(f * level_rows, level_rows)]
            moved_low[pl.ds(f * level_rows * lat_rows, level_rows * lat_rows), :] = both.reshape(
                level_rows * lat_rows, lon_total
            ).astype(jnp.bfloat16)

    small_row = lax.broadcasted_iota(jnp.int32, (lat_rows, LANES), 0)
    mask = jnp.zeros((lat_rows, LANES), jnp.int32)
    for j in range(lat_rows):
        mask = jnp.where(small_row == j, mask_ref[j], mask)

    def owner_of(q):
        rest = jnp.maximum(q - full, 0)
        place = lax.rem(rest, group_size - 1)
        place = place + jnp.where(place >= slot, 1, 0)
        later = full + lax.div(rest, group_size - 1) * group_size + place
        return jnp.where(q < full, q, later)

    def send(q, d):
        @pl.when(d != lev)
        def _():
            lanes = pl.ds(pl.multiple_of(lax.rem(q, tiles) * LANES, LANES), LANES)
            pltpu.make_async_remote_copy(
                src_ref=filtered.at[lax.div(q, tiles), :, :, lanes],
                dst_ref=columns.at[pl.ds(lev * level_rows, level_rows)],
                send_sem=column_send,
                recv_sem=column_recv,
                device_id={"lev": d},
                device_id_type=MESH,
            ).start()

    def send_to(d):
        @pl.when(owns(d))
        def _():
            send(unit_of(d), d)

    far_field = lax.div(
        lax.rem(lev + lev_count // 2, lev_count) * field_count, lev_count
    )

    for first in range(0, tiles, 2):
        count = min(2, tiles - first)
        width = count * LANES
        lanes = pl.ds(first * LANES, width)

        @pl.when(polar)
        def _():
            correction = jnp.dot(
                moved_low[...], matrix_ref[:, lanes], preferred_element_type=jnp.float32
            ).reshape(field_count, level_rows, lat_rows, width)
            wide_mask = jnp.concatenate([mask] * count, axis=1) == 1
            kept = jnp.where(wide_mask[None, None], correction, 0.0)
            total = moved[:, :, lanes].reshape(kept.shape) + kept
            filtered[:, :, :, lanes] = total.astype(jnp.bfloat16)

        @pl.when(jnp.logical_not(polar))
        def _():
            filtered[:, :, :, lanes] = (
                moved[:, :, lanes]
                .reshape(field_count, level_rows, lat_rows, width)
                .astype(jnp.bfloat16)
            )

        def send_block(i, carry):
            f = lax.rem(far_field + i, field_count)
            for k in range(count):
                q = f * tiles + first + k

                @pl.when(owner_of(q) < ready_count)
                def _():
                    send(q, owner_of(q))

            return carry

        lax.fori_loop(0, field_count, send_block, 0)

    def send_later(h, carry):
        pl.semaphore_wait(ready.at[h], group_size)

        def each(k, carry):
            send_to(h * group_size + k)
            return carry

        return lax.fori_loop(0, group_size, each, carry)

    lax.fori_loop(group + 1, groups, send_later, 0)

    @pl.when(active)
    def _():
        group = 8

        def spread_group(g, weights):
            rolled = []
            for b in range(band_width):
                for k in range(group):
                    spread[g * group + k, b] = jnp.broadcast_to(
                        weights[b][:, k : k + 1], (lat_rows, LANES)
                    )
                rolled.append(pltpu.roll(weights[b], LANES - group, 1))
            return tuple(rolled)

        lax.fori_loop(
            0,
            level_total // group,
            spread_group,
            tuple(weight_ref[:, b, :] for b in range(band_width)),
        )

    def sized(count):
        return columns.at[pl.ds(0, count * level_rows)]

    @pl.when(active)
    def _():
        columns[pl.ds(lev * level_rows, level_rows)] = filtered[unit_field, :, :, unit_lanes]
        pltpu.make_async_copy(sized(lev_count - 1), sized(lev_count - 1), column_recv).wait()

        def target(t):
            begin = start_ref[t]
            total = jnp.zeros((lat_rows, LANES), jnp.float32)
            for b in range(band_width):
                total = total + spread[t, b] * columns[begin + b].astype(jnp.float32)
            return total.astype(jnp.bfloat16)

        def send_piece(peer):
            place = pl.ds(peer * level_rows, level_rows)
            for l in range(level_rows):
                remapped[peer * level_rows + l] = target(peer * level_rows + l)
            pltpu.make_async_remote_copy(
                src_ref=remapped.at[place],
                dst_ref=out_ref.at[unit_field, :, :, unit_lanes],
                send_sem=back_send,
                recv_sem=back_recv,
                device_id={"lev": peer},
                device_id_type=MESH,
            ).start()

        late = 3

        def send_back(i, carry):
            place = lax.rem(i, group_size)
            plane = lax.div(i, group_size)
            plane = plane - jnp.where(place == slot, late, jnp.where(place > slot, late - 1, 0))
            peer = plane * group_size + place

            @pl.when((plane >= 0) & (plane < groups) & (peer != lev))
            def _():
                send_piece(peer)

            return carry

        lax.fori_loop(0, lev_count + late * group_size, send_back, 0)
        for l in range(level_rows):
            remapped[lev * level_rows + l] = target(lev * level_rows + l)
        keep = pltpu.make_async_copy(
            remapped.at[pl.ds(lev * level_rows, level_rows)],
            out_ref.at[unit_field, :, :, unit_lanes],
            place_sem,
        )
        keep.start()
        pltpu.make_async_copy(sized(lev_count - 1), sized(lev_count - 1), back_send).wait()
        pltpu.make_async_copy(sized(units - 1), sized(units - 1), column_send).wait()
        pltpu.make_async_copy(sized(units - 1), sized(units - 1), back_recv).wait()
        keep.wait()

    @pl.when(jnp.logical_not(active))
    def _():
        pltpu.make_async_copy(sized(units), sized(units), column_send).wait()
        pltpu.make_async_copy(sized(units), sized(units), back_recv).wait()

    @pl.when(has_high)
    def _():
        for copy in halo_copies(True):
            copy.wait_send()

    @pl.when(has_low)
    def _():
        for copy in halo_copies(False):
            copy.wait_send()


def on_device(lat_count, lev_count, fields, courant, matrix, mask, start, weights):
    field_count, level_rows, lat_rows, lon_total = fields.shape
    planes = field_count * level_rows
    group_size = 4
    level_total = level_rows * lev_count
    band_width = weights.shape[2]
    bf16, f32 = jnp.bfloat16, jnp.float32
    anywhere = pl.BlockSpec(memory_space=pl.ANY)
    return pl.pallas_call(
        functools.partial(
            kernel, lat_count=lat_count, lev_count=lev_count, group_size=group_size
        ),
        out_shape=jax.ShapeDtypeStruct(fields.shape, bf16),
        in_specs=[anywhere] * 6,
        out_specs=anywhere,
        scratch_shapes=[
            pltpu.SMEM(mask.shape, jnp.int32),
            pltpu.SMEM(start.shape, jnp.int32),
            pltpu.VMEM((weights.shape[0], band_width, level_total), f32),
            pltpu.VMEM(fields.shape, bf16),
            pltpu.VMEM(courant.shape, bf16),
            pltpu.VMEM(matrix.shape, bf16),
            pltpu.VMEM((field_count, level_rows, 2, lon_total), bf16),
            pltpu.VMEM((field_count, level_rows, 2, lon_total), bf16),
            pltpu.VMEM((level_rows, 2, lon_total), bf16),
            pltpu.VMEM((level_rows, 2, lon_total), bf16),
            pltpu.VMEM((planes, lat_rows + 16, lon_total), f32),
            pltpu.VMEM((level_rows, lat_rows + 16, lon_total), f32),
            pltpu.VMEM((planes, lat_rows, lon_total), f32),
            pltpu.VMEM((planes * lat_rows, lon_total), bf16),
            pltpu.VMEM(fields.shape, bf16),
            pltpu.VMEM((level_total, lat_rows, LANES), bf16),
            pltpu.VMEM((level_total, band_width, lat_rows, LANES), f32),
            pltpu.VMEM((level_total, lat_rows, LANES), bf16),
            pltpu.SemaphoreType.DMA((6,)),
            pltpu.SemaphoreType.DMA,
            pltpu.SemaphoreType.REGULAR((lev_count // group_size,)),
            pltpu.SemaphoreType.DMA((2, 2)),
            pltpu.SemaphoreType.DMA((2, 2)),
            pltpu.SemaphoreType.DMA,
            pltpu.SemaphoreType.DMA,
            pltpu.SemaphoreType.DMA,
            pltpu.SemaphoreType.DMA,
        ],
        compiler_params=pltpu.CompilerParams(
            collective_id=0, has_side_effects=True, vmem_limit_bytes=63 << 20
        ),
    )(fields, courant, matrix, mask, start, jnp.transpose(weights, (0, 2, 1)))


def solution(mesh):
    step = functools.partial(on_device, mesh.shape["lat"], mesh.shape["lev"])
    placed = (
        P(None, "lev", "lat", None),
        P("lev", "lat", None),
        P(),
        P("lat"),
        P(),
        P("lat", None, None),
    )
    return jax.shard_map(
        step, mesh=mesh, in_specs=placed, out_specs=P(None, "lev", "lat", None), check_vma=False
    )
```
